32 devices in a mesh: table: 2 (over x), batch: 16 (over z, y, core).
Axes of the slice: x: 2, y: 2, z: 4, core: 2. Of those that a mesh axis runs over, the one named last changes fastest.
Arguments:
- x_first: bfloat16 [2048, 4096], P('batch', 'table'), may hold values from -6 to 6
- x_layer: bfloat16 [2048, 4096], P('batch', 'table'), may hold values from -6 to 6
- pre_act: bfloat16 [2048, 4096], P('batch', 'table'), may hold values from -8 to 8
- gamma: float32 [4096], P('table'), may hold values from 0.3 to 3
- weight: float32 [4096, 4096], P('table', 'batch'), may hold values from -0.09375 to 0.09375
- cotangent: bfloat16 [2048, 4096], P('batch', 'table'), may hold values from -12 to 12
Outputs:
- grad_first: bfloat16 [2048, 4096], P('batch', 'table')
- grad_layer: bfloat16 [2048, 4096], P('batch', 'table')
- grad_weight: float32 [4096, 4096], P('table', 'batch')
- grad_bias: float32 [4096], P('table')
- grad_gamma: float32 [4096], P('table')
The draws below stay inside these ranges and needn't reach their ends.
All inputs are finite; a program needn't handle non-finite values.
Results may differ from the reference program's by a relative error of at most 0.005.
Values may be sent and summed in bfloat16 or wider, within the bound.
A program may use at most 128 MiB of HBM per device.

```python
import math
import jax
import jax.numpy as jnp
from jax import lax

D = 4096
SAMPLES = 2048


def draw_cotangent(key, part):
    key_one = jax.random.fold_in(key, 11)
    row_scale = 1.0 + 2.0 * jnp.arange(SAMPLES, dtype=jnp.float32) / SAMPLES
    base = jnp.clip(jax.random.normal(key_one, (SAMPLES, D), jnp.float32), -4.0, 4.0)
    values = base * row_scale[:, None]
    return values.astype(jnp.bfloat16)


def block_levels(key, extent, pieces, least, largest):
    factor_of = 1.0
    for position, parts in pieces:
        draws = jax.random.uniform(jax.random.fold_in(jax.random.fold_in(key, 6), position), (parts,), jnp.float32, least / len(pieces), largest / len(pieces))
        factor_of = factor_of * jnp.repeat(jnp.exp(draws), extent[position] // parts).reshape((-1,) + (1,) * (len(extent) - 1 - position))
    return factor_of


def scatter_about(rng, dims, width, limit, split=(), kind=jnp.bfloat16):
    array = width * jax.random.normal(rng, dims, jnp.float32)
    if split:
        array = array * block_levels(rng, dims, split, -0.22, 0.18)
    return jnp.clip(array, -limit, limit).astype(kind)


def setup_inputs(seed: int = 0) -> dict:
    streams_of = jax.random.split(jax.random.key(seed), 7)
    x_first = scatter_about(streams_of[0], (SAMPLES, D), 1.0, 6.0, ((0, 16), (1, 2)))
    x_layer = scatter_about(streams_of[1], (SAMPLES, D), 1.0, 6.0, ((0, 16), (1, 2)))
    pre_act = scatter_about(streams_of[2], (SAMPLES, D), 1.5, 8.0, ((0, 16), (1, 2)))
    gamma = jnp.clip(jnp.exp(math.log(3.0) - 2.3025851 * jax.random.uniform(streams_of[3], (D,), jnp.float32) ** block_levels(streams_of[3], (D,), ((0, 2),), -0.2, 0.2)), 0.3, 3.0)
    weight = scatter_about(streams_of[4], (D, D), D ** -0.5, 0.09375, ((0, 2), (1, 16)), jnp.float32)
    cotangent = draw_cotangent(jax.random.fold_in(streams_of[6], 71), 0)
    return {"x_first": x_first, "x_layer": x_layer, "pre_act": pre_act, "gamma": gamma, "weight": weight, "cotangent": cotangent}


def reference(x_first, x_layer, pre_act, gamma, weight, cotangent):
    weight_bf = weight.astype(jnp.bfloat16)
    pre_full = pre_act.astype(jnp.float32)
    gate_tanh = jnp.tanh(gamma[None, :] * pre_full)
    hidden = pre_full * gate_tanh
    cot_full = cotangent.astype(jnp.float32)
    grad_hidden = cot_full * x_first.astype(jnp.float32)
    grad_first = (cot_full * hidden).astype(jnp.bfloat16)
    slope = 1.0 - gate_tanh * gate_tanh
    grad_pre = (grad_hidden * (gate_tanh + gamma[None, :] * pre_full * slope)).astype(jnp.bfloat16)
    grad_gamma = jnp.sum(grad_hidden * pre_full * pre_full * slope, axis=0)
    grad_bias = jnp.sum(grad_pre.astype(jnp.float32), axis=0)
    grad_weight = lax.dot_general(grad_pre, x_layer, (((0,), (0,)), ((), ())), preferred_element_type=jnp.float32)
    grad_layer = (cot_full + jnp.dot(grad_pre, weight_bf, preferred_element_type=jnp.float32)).astype(jnp.bfloat16)
    return grad_first, grad_layer, grad_weight, grad_bias, grad_gamma
```

```python
import functools

import jax
import jax.numpy as jnp
from jax import lax
from jax.experimental import pallas as pl
from jax.experimental.pallas import tpu as pltpu
from jax.sharding import PartitionSpec as P

MESH = pl.DeviceIdType.MESH
F32 = jnp.float32
BF16 = jnp.bfloat16


def exchange(
    nt, nb, parts,
    pre_ref, cols_ref, weight_ref, small_ref,
    wsum_ref, ret_ref, total_ref,
    held, xall, shares, smalls, wfull, wbf,
    ring_send, ring_recv, sib_send, sib_recv, own_sem, x_send, x_recv,
    ret_send, ret_recv, small_send, small_recv, w_sem,
):
    rows, outs = pre_ref.shape
    per = nb // nt
    nc = nb // 2
    hops = nc // 2
    part = rows // parts
    t, b = lax.axis_index("table"), lax.axis_index("batch")
    q, c = b // 2, b % 2

    def chip_at(p):
        p = (p + nc) % nc
        return jnp.where(p < hops, 2 * p, 2 * (nc - 1 - p) + 1)

    p = jnp.where(q % 2 == 0, q // 2, nc - 1 - q // 2)
    ahead = [2 * chip_at(p + 1) + c, 2 * chip_at(p - 1) + c]
    origin = lambda d, k: chip_at(p - k if d == 0 else p + k)
    count = lambda d, core: jnp.where(core == d, hops, hops - 1)
    home = b // per
    slot = b % per

    def piece(chip, core, h):
        return held.at[chip, pl.ds(pl.multiple_of(core * rows + h * part, part), part), :]

    def block(ref, bb):
        return ref.at[bb // 2, pl.ds(pl.multiple_of((bb % 2) * rows, rows), rows), :]

    def done(ref, sem):
        pltpu.make_async_copy(ref, ref, sem).wait()

    def send(src, dst, ssem, rsem, tt, bb):
        return pltpu.make_async_remote_copy(
            src_ref=src, dst_ref=dst, send_sem=ssem, recv_sem=rsem, device_id=(tt, bb), device_id_type=MESH
        ).start()

    load_w = pltpu.make_async_copy(weight_ref, wfull, w_sem)
    load_w.start()
    barrier = pltpu.get_barrier_semaphore()

    def greet(i, carry):
        tt, bb = i // nb, i % nb

        @pl.when(jnp.logical_or(tt != t, bb != b))
        def _():
            pl.semaphore_signal(barrier, inc=1, device_id=(tt, bb), device_id_type=MESH)

        return carry

    lax.fori_loop(0, nt * nb, greet, 0)
    pl.semaphore_wait(barrier, nt * nb - 1)

    for h in range(parts):
        mine = pre_ref.at[pl.ds(h * part, part), :]
        for d in range(2):
            @pl.when(count(d, c) > 0)
            def _():
                send(mine, piece(q, c, h), ring_send.at[d, 0, h], ring_recv.at[d, 0, h], t, ahead[d])
    send(pre_ref, block(held, b), own_sem.at[0], own_sem.at[1], t, 2 * q + 1 - c)
    own_copy = pltpu.make_async_copy(pre_ref, block(held, b), own_sem.at[2])
    own_copy.start()

    def give_columns(i, carry):
        tt, j = i % nt, i // nt
        bb = t * per + j
        me = jnp.logical_and(tt == t, bb == b)

        @pl.when(me)
        def _():
            pltpu.make_async_copy(cols_ref.at[j], block(xall, b), x_recv.at[b]).start()

        @pl.when(jnp.logical_not(me))
        def _():
            send(cols_ref.at[j], block(xall, b), x_send.at[i], x_recv.at[b], tt, bb)

        return carry

    lax.fori_loop(0, nb, give_columns, 0)

    def give_small(bb, carry):
        @pl.when(bb != b)
        def _():
            send(small_ref, smalls.at[b], small_send.at[bb], small_recv.at[b], t, bb)

        return carry

    lax.fori_loop(0, nb, give_small, 0)
    load_w.wait()
    wbf[...] = wfull[...].astype(BF16)

    def product(chip):
        shares[chip] = jnp.dot(held[chip], wbf[...], preferred_element_type=F32).astype(BF16)

    def give_shares(chip):
        product(chip)
        for core in range(2):
            bb = 2 * chip + core
            send(block(shares, bb), ret_ref.at[t, slot], ret_send.at[bb], ret_recv.at[t, slot], home, bb)

    wide = 512 if outs % 512 == 0 else outs

    def add_weight(chip, first):
        for core in range(2):
            done(block(xall, 2 * chip + core), x_recv.at[2 * chip + core])

        def step(i, carry):
            at = pl.ds(pl.multiple_of(i * wide, wide), wide)
            term = lax.dot_general(
                held[chip, :, at], xall[chip], (((0,), (0,)), ((), ())), preferred_element_type=F32
            )
            wsum_ref[at, :] = term if first else wsum_ref[at, :] + term
            return carry

        lax.fori_loop(0, outs // wide, step, 0)

    own_copy.wait()
    done(block(held, b), own_sem.at[1])
    product(q)
    for core in range(2):
        bb = 2 * q + core
        me = jnp.logical_and(bb == b, home == t)

        @pl.when(me)
        def _():
            pltpu.make_async_copy(block(shares, bb), ret_ref.at[t, slot], ret_recv.at[t, slot]).start()

        @pl.when(jnp.logical_not(me))
        def _():
            send(block(shares, bb), ret_ref.at[t, slot], ret_send.at[bb], ret_recv.at[t, slot], home, bb)

    add_weight(q, True)

    def hop(k, carry):
        for h in range(parts):
            for d in range(2):
                here = piece(origin(d, k + 1), c, h)

                @pl.when(k < count(d, c))
                def _():
                    done(here, ring_recv.at[d, k, h])

                    @pl.when(k + 1 < count(d, c))
                    def _():
                        send(here, here, ring_send.at[d, k + 1, h], ring_recv.at[d, k + 1, h], t, ahead[d])

                    send(here, here, sib_send.at[d, k, h], sib_recv.at[d, k, h], t, 2 * q + 1 - c)
        for d in range(2):
            @pl.when(k < count(d, 1 - c))
            def _():
                for h in range(parts):
                    done(piece(origin(d, k + 1), 1 - c, h), sib_recv.at[d, k, h])
        give_shares(origin(0, k + 1))

        @pl.when(k < hops - 1)
        def _():
            give_shares(origin(1, k + 1))

        @pl.when(k > 0)
        def _():
            add_weight(origin(0, k), False)
            add_weight(origin(1, k), False)

        return carry

    lax.fori_loop(0, hops, hop, 0)
    add_weight(origin(0, hops), False)

    smalls[b] = small_ref[...]

    def take_small(bb, carry):
        @pl.when(bb != b)
        def _():
            done(smalls.at[bb], small_recv.at[bb])
            done(small_ref, small_send.at[bb])

        return carry

    lax.fori_loop(0, nb, take_small, 0)
    total_ref[...] = jnp.sum(smalls[...], axis=0)

    def sent_columns(i, carry):
        @pl.when(jnp.logical_or(i % nt != t, t * per + i // nt != b))
        def _():
            done(cols_ref.at[i // nt], x_send.at[i])

        return carry

    lax.fori_loop(0, nb, sent_columns, 0)

    def sent_shares(bb, carry):
        @pl.when(jnp.logical_or(bb != b, home != t))
        def _():
            done(block(shares, bb), ret_send.at[bb])

        done(ret_ref.at[bb // per, bb % per], ret_recv.at[bb // per, bb % per])
        return carry

    lax.fori_loop(0, nb, sent_shares, 0)
    done(pre_ref, own_sem.at[0])

    def sent_pieces(k, carry):
        for h in range(parts):
            for d in range(2):
                @pl.when(k < count(d, c))
                def _():
                    done(piece(origin(d, k), c, h), ring_send.at[d, k, h])
                    done(piece(origin(d, k + 1), c, h), sib_send.at[d, k, h])

        return carry

    lax.fori_loop(0, hops, sent_pieces, 0)


def run_exchange(nt, nb, grad_pre, columns, weight, small):
    rows, outs = grad_pre.shape
    cols = weight.shape[1]
    nc, per, hops = nb // 2, nb // nt, max(nb // 4, 1)
    parts = 4 if rows % 64 == 0 else 1
    dma = pltpu.SemaphoreType.DMA
    vmem = pl.BlockSpec(memory_space=pltpu.VMEM)
    return pl.pallas_call(
        functools.partial(exchange, nt, nb, parts),
        out_shape=(
            jax.ShapeDtypeStruct((outs, cols), F32),
            jax.ShapeDtypeStruct((nt, per, rows, cols), BF16),
            jax.ShapeDtypeStruct(small.shape, F32),
        ),
        in_specs=[vmem, vmem, pl.BlockSpec(memory_space=pl.ANY), vmem],
        out_specs=(vmem, vmem, vmem),
        scratch_shapes=[
            pltpu.VMEM((nc, 2 * rows, outs), BF16),
            pltpu.VMEM((nc, 2 * rows, cols), BF16),
            pltpu.VMEM((nc, 2 * rows, cols), BF16),
            pltpu.VMEM((nb,) + small.shape, F32),
            pltpu.VMEM((outs, cols), F32),
            pltpu.VMEM((outs, cols), BF16),
            dma((2, hops, parts)),
            dma((2, hops, parts)),
            dma((2, hops, parts)),
            dma((2, hops, parts)),
            dma((3,)),
            dma((nb,)),
            dma((nb,)),
            dma((nb,)),
            dma((nt, per)),
            dma((nb,)),
            dma((nb,)),
            dma,
        ],
        compiler_params=pltpu.CompilerParams(
            collective_id=0, has_side_effects=True, vmem_limit_bytes=60 * 1024 * 1024
        ),
    )(grad_pre, columns, weight, small)


def shards(nt, nb, x_first, x_layer, pre_act, gamma, weight, cotangent):
    pre_full = pre_act.astype(F32)
    gate_tanh = jnp.tanh(gamma[None, :] * pre_full)
    hidden = pre_full * gate_tanh
    cot_full = cotangent.astype(F32)
    grad_hidden = cot_full * x_first.astype(F32)
    grad_first = (cot_full * hidden).astype(BF16)
    slope = 1.0 - gate_tanh * gate_tanh
    grad_pre = (grad_hidden * (gate_tanh + gamma[None, :] * pre_full * slope)).astype(BF16)
    local_gamma = jnp.sum(grad_hidden * pre_full * pre_full * slope, axis=0)
    local_bias = jnp.sum(grad_pre.astype(F32), axis=0)
    small = jnp.stack([local_bias, local_gamma])
    rows = x_layer.shape[0]
    per = nb // nt
    columns = x_layer.reshape(rows, per, -1).transpose(1, 0, 2)
    grad_weight, returned, total = run_exchange(nt, nb, grad_pre, columns, weight, small)
    share = jnp.sum(returned.astype(F32), axis=0).transpose(1, 0, 2).reshape(rows, -1)
    grad_layer = (cot_full + share).astype(BF16)
    return (grad_first, grad_layer, grad_weight, total[0], total[1])


def solution(mesh):
    placed = (
        P("batch", "table"),
        P("batch", "table"),
        P("batch", "table"),
        P("table"),
        P("table", "batch"),
        P("batch", "table"),
    )
    return jax.shard_map(
        functools.partial(shards, mesh.shape["table"], mesh.shape["batch"]),
        mesh=mesh,
        in_specs=placed,
        out_specs=(
            P("batch", "table"),
            P("batch", "table"),
            P("table", "batch"),
            P("table"),
            P("table"),
        ),
        check_vma=False,
    )
```

```python
import functools

import jax
import jax.numpy as jnp
from jax import lax
from jax.experimental import pallas as pl
from jax.experimental.pallas import tpu as pltpu
from jax.sharding import PartitionSpec as P

MESH = pl.DeviceIdType.MESH
F32 = jnp.float32
BF16 = jnp.bfloat16


def exchange(
    nb, parts,
    pre_ref, cols_ref, weight_ref, small_ref,
    wsum_ref, ret_ref, total_ref,
    held, xall, mine, theirs, inbox, summed, layover, smalls, wfull, wbf,
    ring_send, ring_recv, sib_send, sib_recv, own_sem, x_send, x_on, x_recv,
    pair_send, pair_recv, sum_send, lay_recv, lay_send, ret_recv, small_send, small_recv, w_sem,
):
    rows, outs = pre_ref.shape
    per = nb // 2
    nc = nb // 2
    hops = nc // 2
    part = rows // parts
    t, b = lax.axis_index("table"), lax.axis_index("batch")
    q, c = b // 2, b % 2
    other = 1 - t

    def chip_at(p):
        p = (p + nc) % nc
        return jnp.where(p < hops, 2 * p, 2 * (nc - 1 - p) + 1)

    p = jnp.where(q % 2 == 0, q // 2, nc - 1 - q // 2)
    ahead = [2 * chip_at(p + 1) + c, 2 * chip_at(p - 1) + c]
    origin = lambda d, k: chip_at(p - k if d == 0 else p + k)
    count = lambda d, core: jnp.where(core == d, hops, hops - 1)
    home = b // per
    slot = b % per

    def piece(chip, core, h):
        return held.at[chip, pl.ds(pl.multiple_of(core * rows + h * part, part), part), :]

    def block(ref, bb):
        return ref.at[bb // 2, pl.ds(pl.multiple_of((bb % 2) * rows, rows), rows), :]

    def done(ref, sem):
        pltpu.make_async_copy(ref, ref, sem).wait()

    def send(src, dst, ssem, rsem, tt, bb):
        return pltpu.make_async_remote_copy(
            src_ref=src, dst_ref=dst, send_sem=ssem, recv_sem=rsem, device_id=(tt, bb), device_id_type=MESH
        ).start()

    def each(k, act):
        act(origin(0, k))

        @pl.when(jnp.logical_and(k > 0, k < hops))
        def _():
            act(origin(1, k))

    load_w = pltpu.make_async_copy(weight_ref, wfull, w_sem)
    load_w.start()
    barrier = pltpu.get_barrier_semaphore()

    def greet(i, carry):
        tt, bb = i // nb, i % nb

        @pl.when(jnp.logical_or(tt != t, bb != b))
        def _():
            pl.semaphore_signal(barrier, inc=1, device_id=(tt, bb), device_id_type=MESH)

        return carry

    lax.fori_loop(0, 2 * nb, greet, 0)
    pl.semaphore_wait(barrier, 2 * nb - 1)

    for h in range(parts):
        start = pre_ref.at[pl.ds(h * part, part), :]
        for d in range(2):
            @pl.when(count(d, c) > 0)
            def _():
                send(start, piece(q, c, h), ring_send.at[d, 0, h], ring_recv.at[d, 0, h], t, ahead[d])
    send(pre_ref, block(held, b), own_sem.at[0], own_sem.at[1], t, 2 * q + 1 - c)
    own_copy = pltpu.make_async_copy(pre_ref, block(held, b), own_sem.at[2])
    own_copy.start()

    first = (t + b) % 2

    def give_columns(j, carry):
        bb = t * per + (j + slot) % per
        me = jnp.logical_and(first == t, bb == b)
        own = cols_ref.at[(j + slot) % per]

        @pl.when(me)
        def _():
            pltpu.make_async_copy(own, block(xall, b), x_recv.at[b]).start()

        @pl.when(jnp.logical_not(me))
        def _():
            send(own, block(xall, b), x_send.at[j], x_recv.at[b], first, bb)

        return carry

    lax.fori_loop(0, per, give_columns, 0)

    def give_small(bb, carry):
        @pl.when(bb != b)
        def _():
            send(small_ref, smalls.at[b], small_send.at[bb], small_recv.at[b], t, bb)

        return carry

    lax.fori_loop(0, nb, give_small, 0)
    load_w.wait()
    wbf[...] = wfull[...].astype(BF16)
    wsum_ref[...] = jnp.zeros_like(wsum_ref)

    def lands_here(bb):
        return (home + bb) % 2 == t

    def pass_columns(chip):
        for core in range(2):
            bb = 2 * chip + core

            @pl.when(lands_here(bb))
            def _():
                done(block(xall, bb), x_recv.at[bb])
                send(block(xall, bb), block(xall, bb), x_on.at[bb], x_recv.at[bb], other, b)

    def half(chip, which):
        at = pl.ds(pl.multiple_of(which * rows, rows), rows)
        return jnp.dot(held[chip, at, :], wbf[...], preferred_element_type=F32)

    def multiply(chip):
        theirs[chip] = half(chip, other).astype(BF16)
        send(theirs.at[chip], inbox.at[chip], pair_send.at[chip], pair_recv.at[chip], other, b)
        mine[chip] = half(chip, t)

    def give_sum(chip):
        done(inbox.at[chip], pair_recv.at[chip])
        summed[chip] = (mine[chip] + inbox[chip].astype(F32)).astype(BF16)
        bb = 2 * chip + t
        for stays, dst, rsem in ((True, ret_ref, ret_recv), (False, layover, lay_recv)):
            right = (home == t) if stays else (home != t)

            @pl.when(jnp.logical_and(right, bb == b))
            def _():
                pltpu.make_async_copy(summed.at[chip], dst.at[slot], rsem.at[slot]).start()

            @pl.when(jnp.logical_and(right, bb != b))
            def _():
                send(summed.at[chip], dst.at[slot], sum_send.at[chip], rsem.at[slot], t, bb)

    def pass_sum(chip):
        for core in range(2):
            bb = 2 * chip + core
            j = bb % per

            @pl.when(jnp.logical_and(c == t, bb // per != t))
            def _():
                done(layover.at[j], lay_recv.at[j])
                send(layover.at[j], ret_ref.at[j], lay_send.at[j], ret_recv.at[j], other, b)

    wide = 512 if outs % 512 == 0 else outs

    def add_weight(chip):
        for core in range(2):
            bb = 2 * chip + core

            @pl.when(jnp.logical_not(lands_here(bb)))
            def _():
                done(block(xall, bb), x_recv.at[bb])

        def step(i, carry):
            at = pl.ds(pl.multiple_of(i * wide, wide), wide)
            wsum_ref[at, :] += lax.dot_general(
                held[chip, :, at], xall[chip], (((0,), (0,)), ((), ())), preferred_element_type=F32
            )
            return carry

        lax.fori_loop(0, outs // wide, step, 0)

    own_copy.wait()
    done(block(held, b), own_sem.at[1])
    multiply(q)
    pass_columns(q)

    def hop(k, carry):
        for h in range(parts):
            for d in range(2):
                here = piece(origin(d, k + 1), c, h)

                @pl.when(k < count(d, c))
                def _():
                    done(here, ring_recv.at[d, k, h])

                    @pl.when(k + 1 < count(d, c))
                    def _():
                        send(here, here, ring_send.at[d, k + 1, h], ring_recv.at[d, k + 1, h], t, ahead[d])

                    send(here, here, sib_send.at[d, k, h], sib_recv.at[d, k, h], t, 2 * q + 1 - c)
        each(k, give_sum)
        each(k + 1, pass_columns)
        for d in range(2):
            @pl.when(k < count(d, 1 - c))
            def _():
                for h in range(parts):
                    done(piece(origin(d, k + 1), 1 - c, h), sib_recv.at[d, k, h])
        each(k + 1, multiply)

        @pl.when(k > 0)
        def _():
            each(k - 1, pass_sum)

        each(k, add_weight)
        return carry

    lax.fori_loop(0, hops, hop, 0)
    each(hops, give_sum)
    each(hops - 1, pass_sum)
    each(hops, add_weight)
    each(hops, pass_sum)

    smalls[b] = small_ref[...]

    def take_small(bb, carry):
        @pl.when(bb != b)
        def _():
            done(smalls.at[bb], small_recv.at[bb])
            done(small_ref, small_send.at[bb])

        return carry

    lax.fori_loop(0, nb, take_small, 0)
    total_ref[...] = jnp.sum(smalls[...], axis=0)

    def sent_columns(j, carry):
        @pl.when(jnp.logical_or(first != t, t * per + (j + slot) % per != b))
        def _():
            done(cols_ref.at[j], x_send.at[j])

        return carry

    lax.fori_loop(0, per, sent_columns, 0)

    def sent_on(bb, carry):
        @pl.when(lands_here(bb))
        def _():
            done(block(xall, bb), x_on.at[bb])

        return carry

    lax.fori_loop(0, nb, sent_on, 0)

    def sent_sums(chip, carry):
        done(theirs.at[chip], pair_send.at[chip])

        @pl.when(2 * chip + t != b)
        def _():
            done(summed.at[chip], sum_send.at[chip])

        return carry

    lax.fori_loop(0, nc, sent_sums, 0)

    def came(j, carry):
        done(ret_ref.at[j], ret_recv.at[j])

        @pl.when(c == t)
        def _():
            done(layover.at[j], lay_send.at[j])

        return carry

    lax.fori_loop(0, per, came, 0)
    done(pre_ref, own_sem.at[0])

    def sent_pieces(k, carry):
        for h in range(parts):
            for d in range(2):
                @pl.when(k < count(d, c))
                def _():
                    done(piece(origin(d, k), c, h), ring_send.at[d, k, h])
                    done(piece(origin(d, k + 1), c, h), sib_send.at[d, k, h])

        return carry

    lax.fori_loop(0, hops, sent_pieces, 0)


def run_exchange(nb, grad_pre, columns, weight, small):
    rows, outs = grad_pre.shape
    cols = weight.shape[1]
    nc, per, hops = nb // 2, nb // 2, nb // 4
    parts = 4 if rows % 64 == 0 else 1
    dma = pltpu.SemaphoreType.DMA
    vmem = pl.BlockSpec(memory_space=pltpu.VMEM)
    return pl.pallas_call(
        functools.partial(exchange, nb, parts),
        out_shape=(
            jax.ShapeDtypeStruct((outs, cols), F32),
            jax.ShapeDtypeStruct((per, rows, cols), BF16),
            jax.ShapeDtypeStruct(small.shape, F32),
        ),
        in_specs=[vmem, vmem, pl.BlockSpec(memory_space=pl.ANY), vmem],
        out_specs=(vmem, vmem, vmem),
        scratch_shapes=[
            pltpu.VMEM((nc, 2 * rows, outs), BF16),
            pltpu.VMEM((nc, 2 * rows, cols), BF16),
            pltpu.VMEM((nc, rows, cols), F32),
            pltpu.VMEM((nc, rows, cols), BF16),
            pltpu.VMEM((nc, rows, cols), BF16),
            pltpu.VMEM((nc, rows, cols), BF16),
            pltpu.VMEM((per, rows, cols), BF16),
            pltpu.VMEM((nb,) + small.shape, F32),
            pltpu.VMEM((outs, cols), F32),
            pltpu.VMEM((outs, cols), BF16),
            dma((2, hops, parts)),
            dma((2, hops, parts)),
            dma((2, hops, parts)),
            dma((2, hops, parts)),
            dma((3,)),
            dma((per,)),
            dma((nb,)),
            dma((nb,)),
            dma((nc,)),
            dma((nc,)),
            dma((nc,)),
            dma((per,)),
            dma((per,)),
            dma((per,)),
            dma((nb,)),
            dma((nb,)),
            dma,
        ],
        compiler_params=pltpu.CompilerParams(
            collective_id=0, has_side_effects=True, vmem_limit_bytes=60 * 1024 * 1024
        ),
    )(grad_pre, columns, weight, small)


def shards(nb, x_first, x_layer, pre_act, gamma, weight, cotangent):
    pre_full = pre_act.astype(F32)
    gate_tanh = jnp.tanh(gamma[None, :] * pre_full)
    hidden = pre_full * gate_tanh
    cot_full = cotangent.astype(F32)
    grad_hidden = cot_full * x_first.astype(F32)
    grad_first = (cot_full * hidden).astype(BF16)
    slope = 1.0 - gate_tanh * gate_tanh
    grad_pre = (grad_hidden * (gate_tanh + gamma[None, :] * pre_full * slope)).astype(BF16)
    local_gamma = jnp.sum(grad_hidden * pre_full * pre_full * slope, axis=0)
    local_bias = jnp.sum(grad_pre.astype(F32), axis=0)
    small = jnp.stack([local_bias, local_gamma])
    rows = x_layer.shape[0]
    per = nb // 2
    columns = x_layer.reshape(rows, per, -1).transpose(1, 0, 2)
    grad_weight, returned, total = run_exchange(nb, grad_pre, columns, weight, small)
    share = returned.astype(F32).transpose(1, 0, 2).reshape(rows, -1)
    grad_layer = (cot_full + share).astype(BF16)
    return (grad_first, grad_layer, grad_weight, total[0], total[1])


def solution(mesh):
    assert mesh.shape["table"] == 2 and mesh.shape["batch"] % 4 == 0
    placed = (
        P("batch", "table"),
        P("batch", "table"),
        P("batch", "table"),
        P("table"),
        P("table", "batch"),
        P("batch", "table"),
    )
    return jax.shard_map(
        functools.partial(shards, mesh.shape["batch"]),
        mesh=mesh,
        in_specs=placed,
        out_specs=(
            P("batch", "table"),
            P("batch", "table"),
            P("table", "batch"),
            P("table"),
            P("table"),
        ),
        check_vma=False,
    )
```

```python
import functools

import jax
import jax.numpy as jnp
from jax import lax
from jax.experimental import pallas as pl
from jax.experimental.pallas import tpu as pltpu
from jax.sharding import PartitionSpec as P

MESH = pl.DeviceIdType.MESH
F32 = jnp.float32
BF16 = jnp.bfloat16


def exchange(
    nb, parts,
    pre_ref, cols_ref, weight_ref, bias_ref, gamma_ref,
    wsum_ref, ret_ref, total_ref,
    held, xall, mine, theirs, inbox, summed, layover, guest, small_ref, smalls, wfull, wbf,
    ring_send, ring_recv, sib_send, sib_recv, own_sem, x_send, x_on, x_recv, swap,
    pair_send, pair_recv, sum_send, lay_recv, lay_send, ret_recv, small_send, small_recv, w_sem,
):
    rows, outs = pre_ref.shape
    per = nb // 2
    nc = nb // 2
    hops = nc // 2
    part = rows // parts
    t, b = lax.axis_index("table"), lax.axis_index("batch")
    q, c = b // 2, b % 2
    other = 1 - t

    def chip_at(p):
        p = (p + nc) % nc
        return jnp.where(p < hops, 2 * p, 2 * (nc - 1 - p) + 1)

    p = jnp.where(q % 2 == 0, q // 2, nc - 1 - q // 2)
    ahead = [2 * chip_at(p + 1) + c, 2 * chip_at(p - 1) + c]
    origin = lambda d, k: chip_at(p - k if d == 0 else p + k)
    count = lambda d, core: jnp.where(core == d, hops, hops - 1)
    home = b // per
    slot = b % per

    def piece(chip, core, h):
        return held.at[chip, pl.ds(pl.multiple_of(core * rows + h * part, part), part), :]

    def block(ref, bb):
        return ref.at[bb // 2, pl.ds(pl.multiple_of((bb % 2) * rows, rows), rows), :]

    def features(ref, j):
        cols = wfull.shape[1]
        return ref.at[j] if len(ref.shape) == 3 else ref.at[:, pl.ds(pl.multiple_of(j * cols, cols), cols)]

    def done(ref, sem):
        pltpu.make_async_copy(ref, ref, sem).wait()

    def send(src, dst, ssem, rsem, tt, bb):
        return pltpu.make_async_remote_copy(
            src_ref=src, dst_ref=dst, send_sem=ssem, recv_sem=rsem, device_id=(tt, bb), device_id_type=MESH
        ).start()

    def each(k, act):
        act(origin(0, k))

        @pl.when(jnp.logical_and(k > 0, k < hops))
        def _():
            act(origin(1, k))

    load_w = pltpu.make_async_copy(weight_ref, wfull, w_sem)
    load_w.start()
    small_ref[0:1, :] = bias_ref[...]
    small_ref[1:2, :] = gamma_ref[...]
    barrier = pltpu.get_barrier_semaphore()

    def greet(i, carry):
        tt, bb = i // nb, i % nb

        @pl.when(jnp.logical_or(tt != t, bb != b))
        def _():
            pl.semaphore_signal(barrier, inc=1, device_id=(tt, bb), device_id_type=MESH)

        return carry

    lax.fori_loop(0, 2 * nb, greet, 0)
    pl.semaphore_wait(barrier, 2 * nb - 1)

    for h in range(parts):
        start = pre_ref.at[pl.ds(h * part, part), :]
        for d in range(2):
            @pl.when(count(d, c) > 0)
            def _():
                send(start, piece(q, c, h), ring_send.at[d, 0, h], ring_recv.at[d, 0, h], t, ahead[d])
    send(pre_ref, block(held, b), own_sem.at[0], own_sem.at[1], t, 2 * q + 1 - c)
    own_copy = pltpu.make_async_copy(pre_ref, block(held, b), own_sem.at[2])
    own_copy.start()

    odd = b % 2 == 1
    side = jnp.where(odd, other, t)

    def give_columns(source):
        def give(j, carry):
            at = (j + slot) % per
            bb = side * per + at

            @pl.when(bb == b)
            def _():
                pltpu.make_async_copy(features(source, at), block(xall, b), x_recv.at[b]).start()

            @pl.when(bb != b)
            def _():
                send(features(source, at), block(xall, b), x_send.at[at], x_recv.at[b], t, bb)

            return carry

        lax.fori_loop(0, per, give, 0)

    @pl.when(odd)
    def _():
        send(cols_ref, guest, swap.at[0], swap.at[1], other, b)

    @pl.when(jnp.logical_not(odd))
    def _():
        give_columns(cols_ref)

    def give_small(bb, carry):
        @pl.when(bb != b)
        def _():
            send(small_ref, smalls.at[b], small_send.at[bb], small_recv.at[b], t, bb)

        return carry

    lax.fori_loop(0, nb, give_small, 0)
    load_w.wait()
    wbf[...] = wfull[...].astype(BF16)
    wsum_ref[...] = jnp.zeros_like(wsum_ref)

    def lands_here(bb):
        return (home + bb) % 2 == t

    def pass_columns(chip):
        for core in range(2):
            bb = 2 * chip + core

            @pl.when(lands_here(bb))
            def _():
                done(block(xall, bb), x_recv.at[bb])
                send(block(xall, bb), block(xall, bb), x_on.at[bb], x_recv.at[bb], other, b)

    def half(chip, which):
        at = pl.ds(pl.multiple_of(which * rows, rows), rows)
        return jnp.dot(held[chip, at, :], wbf[...], preferred_element_type=F32)

    def multiply(chip):
        theirs[chip] = half(chip, other).astype(BF16)
        send(theirs.at[chip], inbox.at[chip], pair_send.at[chip], pair_recv.at[chip], other, b)
        mine[chip] = half(chip, t)

    def give_sum(chip):
        done(inbox.at[chip], pair_recv.at[chip])
        summed[chip] = (mine[chip] + inbox[chip].astype(F32)).astype(BF16)
        bb = 2 * chip + t
        for stays, dst, rsem in ((True, ret_ref, ret_recv), (False, layover, lay_recv)):
            right = (home == t) if stays else (home != t)

            @pl.when(jnp.logical_and(right, bb == b))
            def _():
                pltpu.make_async_copy(summed.at[chip], features(dst, slot), rsem.at[slot]).start()

            @pl.when(jnp.logical_and(right, bb != b))
            def _():
                send(summed.at[chip], features(dst, slot), sum_send.at[chip], rsem.at[slot], t, bb)

    def pass_sum(chip):
        for core in range(2):
            bb = 2 * chip + core
            j = bb % per

            @pl.when(jnp.logical_and(c == t, bb // per != t))
            def _():
                done(layover.at[j], lay_recv.at[j])
                send(layover.at[j], features(ret_ref, j), lay_send.at[j], ret_recv.at[j], other, b)

    wide = 512 if outs % 512 == 0 else outs

    def add_weight(chip):
        for core in range(2):
            bb = 2 * chip + core

            @pl.when(jnp.logical_not(lands_here(bb)))
            def _():
                done(block(xall, bb), x_recv.at[bb])

        def step(i, carry):
            at = pl.ds(pl.multiple_of(i * wide, wide), wide)
            wsum_ref[at, :] += lax.dot_general(
                held[chip, :, at], xall[chip], (((0,), (0,)), ((), ())), preferred_element_type=F32
            )
            return carry

        lax.fori_loop(0, outs // wide, step, 0)

    own_copy.wait()
    done(block(held, b), own_sem.at[1])
    multiply(q)

    @pl.when(odd)
    def _():
        done(guest, swap.at[1])
        give_columns(guest)

    pass_columns(q)

    def hop(k, carry):
        for h in range(parts):
            for d in range(2):
                here = piece(origin(d, k + 1), c, h)

                @pl.when(k < count(d, c))
                def _():
                    done(here, ring_recv.at[d, k, h])

                    @pl.when(k + 1 < count(d, c))
                    def _():
                        send(here, here, ring_send.at[d, k + 1, h], ring_recv.at[d, k + 1, h], t, ahead[d])

                    send(here, here, sib_send.at[d, k, h], sib_recv.at[d, k, h], t, 2 * q + 1 - c)
        each(k, give_sum)
        each(k + 1, pass_columns)
        for d in range(2):
            @pl.when(k < count(d, 1 - c))
            def _():
                for h in range(parts):
                    done(piece(origin(d, k + 1), 1 - c, h), sib_recv.at[d, k, h])
        each(k + 1, multiply)

        @pl.when(k > 0)
        def _():
            each(k - 1, pass_sum)

        each(k, add_weight)
        return carry

    lax.fori_loop(0, hops, hop, 0)
    each(hops, give_sum)
    each(hops - 1, pass_sum)
    each(hops, add_weight)
    each(hops, pass_sum)

    smalls[b] = small_ref[...]

    def take_small(bb, carry):
        @pl.when(bb != b)
        def _():
            done(smalls.at[bb], small_recv.at[bb])
            done(small_ref, small_send.at[bb])

        return carry

    lax.fori_loop(0, nb, take_small, 0)
    total_ref[...] = jnp.sum(smalls[...], axis=0)

    @pl.when(odd)
    def _():
        done(cols_ref, swap.at[0])

    def sent_columns(j, carry):
        @pl.when(side * per + j != b)
        def _():
            done(features(cols_ref, j), x_send.at[j])

        return carry

    lax.fori_loop(0, per, sent_columns, 0)

    def sent_on(bb, carry):
        @pl.when(lands_here(bb))
        def _():
            done(block(xall, bb), x_on.at[bb])

        return carry

    lax.fori_loop(0, nb, sent_on, 0)

    def sent_sums(chip, carry):
        done(theirs.at[chip], pair_send.at[chip])

        @pl.when(2 * chip + t != b)
        def _():
            done(summed.at[chip], sum_send.at[chip])

        return carry

    lax.fori_loop(0, nc, sent_sums, 0)

    def came(j, carry):
        done(features(ret_ref, j), ret_recv.at[j])

        @pl.when(c == t)
        def _():
            done(layover.at[j], lay_send.at[j])

        return carry

    lax.fori_loop(0, per, came, 0)
    done(pre_ref, own_sem.at[0])

    def sent_pieces(k, carry):
        for h in range(parts):
            for d in range(2):
                @pl.when(k < count(d, c))
                def _():
                    done(piece(origin(d, k), c, h), ring_send.at[d, k, h])
                    done(piece(origin(d, k + 1), c, h), sib_send.at[d, k, h])

        return carry

    lax.fori_loop(0, hops, sent_pieces, 0)


def run_exchange(nb, grad_pre, columns, weight, bias, gamma):
    rows, outs = grad_pre.shape
    cols = weight.shape[1]
    nc, per, hops = nb // 2, nb // 2, nb // 4
    parts = 4 if rows % 64 == 0 else 1
    dma = pltpu.SemaphoreType.DMA
    vmem = pl.BlockSpec(memory_space=pltpu.VMEM)
    return pl.pallas_call(
        functools.partial(exchange, nb, parts),
        out_shape=(
            jax.ShapeDtypeStruct((outs, cols), F32),
            jax.ShapeDtypeStruct(columns.shape, BF16),
            jax.ShapeDtypeStruct((2, outs), F32),
        ),
        in_specs=[vmem, vmem, pl.BlockSpec(memory_space=pl.ANY), vmem, vmem],
        out_specs=(vmem, vmem, vmem),
        scratch_shapes=[
            pltpu.VMEM((nc, 2 * rows, outs), BF16),
            pltpu.VMEM((nc, 2 * rows, cols), BF16),
            pltpu.VMEM((nc, rows, cols), F32),
            pltpu.VMEM((nc, rows, cols), BF16),
            pltpu.VMEM((nc, rows, cols), BF16),
            pltpu.VMEM((nc, rows, cols), BF16),
            pltpu.VMEM((per, rows, cols), BF16),
            pltpu.VMEM(columns.shape, BF16),
            pltpu.VMEM((2, outs), F32),
            pltpu.VMEM((nb, 2, outs), F32),
            pltpu.VMEM((outs, cols), F32),
            pltpu.VMEM((outs, cols), BF16),
            dma((2, hops, parts)),
            dma((2, hops, parts)),
            dma((2, hops, parts)),
            dma((2, hops, parts)),
            dma((3,)),
            dma((per,)),
            dma((nb,)),
            dma((nb,)),
            dma((2,)),
            dma((nc,)),
            dma((nc,)),
            dma((nc,)),
            dma((per,)),
            dma((per,)),
            dma((per,)),
            dma((nb,)),
            dma((nb,)),
            dma,
        ],
        compiler_params=pltpu.CompilerParams(
            collective_id=0, has_side_effects=True, vmem_limit_bytes=60 * 1024 * 1024
        ),
    )(grad_pre, columns, weight, bias, gamma)


def shards(nb, x_first, x_layer, pre_act, gamma, weight, cotangent):
    pre_full = pre_act.astype(F32)
    gate_tanh = jnp.tanh(gamma[None, :] * pre_full)
    hidden = pre_full * gate_tanh
    cot_full = cotangent.astype(F32)
    grad_hidden = cot_full * x_first.astype(F32)
    grad_first = (cot_full * hidden).astype(BF16)
    slope = 1.0 - gate_tanh * gate_tanh
    grad_pre = (grad_hidden * (gate_tanh + gamma[None, :] * pre_full * slope)).astype(BF16)
    local_gamma = jnp.sum(grad_hidden * pre_full * pre_full * slope, axis=0)
    local_bias = jnp.sum(grad_pre.astype(F32), axis=0)
    rows = x_layer.shape[0]
    per, cols = nb // 2, weight.shape[1]
    aligned = cols % 128 == 0
    columns = x_layer if aligned else x_layer.reshape(rows, per, cols).transpose(1, 0, 2)
    grad_weight, share, total = run_exchange(nb, grad_pre, columns, weight, local_bias[None], local_gamma[None])
    if not aligned:
        share = share.transpose(1, 0, 2).reshape(rows, per * cols)
    grad_layer = (cot_full + share.astype(F32)).astype(BF16)
    return (grad_first, grad_layer, grad_weight, total[0], total[1])


def solution(mesh):
    assert mesh.shape["table"] == 2 and mesh.shape["batch"] % 4 == 0
    placed = (
        P("batch", "table"),
        P("batch", "table"),
        P("batch", "table"),
        P("table"),
        P("table", "batch"),
        P("batch", "table"),
    )
    return jax.shard_map(
        functools.partial(shards, mesh.shape["batch"]),
        mesh=mesh,
        in_specs=placed,
        out_specs=(
            P("batch", "table"),
            P("batch", "table"),
            P("table", "batch"),
            P("table"),
            P("table"),
        ),
        check_vma=False,
    )
```

```python
import functools

import jax
import jax.numpy as jnp
from jax import lax
from jax.experimental import pallas as pl
from jax.experimental.pallas import tpu as pltpu
from jax.sharding import PartitionSpec as P

MESH = pl.DeviceIdType.MESH
F32 = jnp.float32
BF16 = jnp.bfloat16


def exchange(
    nb, parts,
    x_ref, act_ref, cot_ref, gamma_ref, cols_ref, weight_ref,
    first_ref, wsum_ref, ret_ref, total_ref,
    pre_ref, held, xall, mine, theirs, inbox, summed, layover, guest, small_ref, smalls, wfull, wbf,
    ring_send, ring_recv, sib_send, sib_recv, own_sem, x_send, x_on, x_recv, swap,
    pair_send, pair_recv, sum_send, lay_recv, lay_send, ret_recv, small_send, small_recv, w_sem,
):
    rows, outs = x_ref.shape
    per = nb // 2
    nc = nb // 2
    hops = nc // 2
    part = rows // parts
    t, b = lax.axis_index("table"), lax.axis_index("batch")
    q, c = b // 2, b % 2
    other = 1 - t

    def chip_at(p):
        p = (p + nc) % nc
        return jnp.where(p < hops, 2 * p, 2 * (nc - 1 - p) + 1)

    p = jnp.where(q % 2 == 0, q // 2, nc - 1 - q // 2)
    ahead = [2 * chip_at(p + 1) + c, 2 * chip_at(p - 1) + c]
    origin = lambda d, k: chip_at(p - k if d == 0 else p + k)
    count = lambda d, core: jnp.where(core == d, hops, hops - 1)
    home = b // per
    slot = b % per

    def piece(chip, core, h):
        return held.at[chip, pl.ds(pl.multiple_of(core * rows + h * part, part), part), :]

    def block(ref, bb):
        return ref.at[bb // 2, pl.ds(pl.multiple_of((bb % 2) * rows, rows), rows), :]

    def features(ref, j):
        cols = wfull.shape[1]
        return ref.at[j] if len(ref.shape) == 3 else ref.at[:, pl.ds(pl.multiple_of(j * cols, cols), cols)]

    def done(ref, sem):
        pltpu.make_async_copy(ref, ref, sem).wait()

    def send(src, dst, ssem, rsem, tt, bb):
        return pltpu.make_async_remote_copy(
            src_ref=src, dst_ref=dst, send_sem=ssem, recv_sem=rsem, device_id=(tt, bb), device_id_type=MESH
        ).start()

    def each(k, act):
        act(origin(0, k))

        @pl.when(jnp.logical_and(k > 0, k < hops))
        def _():
            act(origin(1, k))

    load_w = pltpu.make_async_copy(weight_ref, wfull, w_sem)
    load_w.start()
    barrier = pltpu.get_barrier_semaphore()

    def greet(i, carry):
        tt, bb = i // nb, i % nb

        @pl.when(jnp.logical_or(tt != t, bb != b))
        def _():
            pl.semaphore_signal(barrier, inc=1, device_id=(tt, bb), device_id_type=MESH)

        return carry

    lax.fori_loop(0, 2 * nb, greet, 0)
    small_ref[...] = jnp.zeros_like(small_ref)
    wide = 512 if outs % 512 == 0 else outs

    def gate(i, carry):
        at = pl.ds(pl.multiple_of(i * part, part), part)
        for lane in range(0, outs, wide):
            to = pl.ds(lane, wide)
            sharp = gamma_ref[:, to]
            act = act_ref[at, to].astype(F32)
            cot = cot_ref[at, to].astype(F32)
            tanh = jnp.tanh(sharp * act)
            hidden = cot * x_ref[at, to].astype(F32)
            slope = 1.0 - tanh * tanh
            first_ref[at, to] = (cot * (act * tanh)).astype(BF16)
            pre = (hidden * (tanh + sharp * act * slope)).astype(BF16)
            pre_ref[at, to] = pre
            small_ref[0:1, to] += jnp.sum(pre.astype(F32), axis=0, keepdims=True)
            small_ref[1:2, to] += jnp.sum(hidden * act * act * slope, axis=0, keepdims=True)
        return carry

    lax.fori_loop(0, parts, gate, 0)
    pl.semaphore_wait(barrier, 2 * nb - 1)

    for h in range(parts):
        start = pre_ref.at[pl.ds(h * part, part), :]
        for d in range(2):
            @pl.when(count(d, c) > 0)
            def _():
                send(start, piece(q, c, h), ring_send.at[d, 0, h], ring_recv.at[d, 0, h], t, ahead[d])
    send(pre_ref, block(held, b), own_sem.at[0], own_sem.at[1], t, 2 * q + 1 - c)
    own_copy = pltpu.make_async_copy(pre_ref, block(held, b), own_sem.at[2])
    own_copy.start()

    odd = b % 2 == 1
    side = jnp.where(odd, other, t)

    def give_columns(source):
        def give(j, carry):
            at = (j + slot) % per
            bb = side * per + at

            @pl.when(bb == b)
            def _():
                pltpu.make_async_copy(features(source, at), block(xall, b), x_recv.at[b]).start()

            @pl.when(bb != b)
            def _():
                send(features(source, at), block(xall, b), x_send.at[at], x_recv.at[b], t, bb)

            return carry

        lax.fori_loop(0, per, give, 0)

    @pl.when(odd)
    def _():
        send(cols_ref, guest, swap.at[0], swap.at[1], other, b)

    @pl.when(jnp.logical_not(odd))
    def _():
        give_columns(cols_ref)

    def give_small(bb, carry):
        @pl.when(bb != b)
        def _():
            send(small_ref, smalls.at[b], small_send.at[bb], small_recv.at[b], t, bb)

        return carry

    lax.fori_loop(0, nb, give_small, 0)
    load_w.wait()
    wbf[...] = wfull[...].astype(BF16)
    wsum_ref[...] = jnp.zeros_like(wsum_ref)

    def lands_here(bb):
        return (home + bb) % 2 == t

    def pass_columns(chip):
        for core in range(2):
            bb = 2 * chip + core

            @pl.when(lands_here(bb))
            def _():
                done(block(xall, bb), x_recv.at[bb])
                send(block(xall, bb), block(xall, bb), x_on.at[bb], x_recv.at[bb], other, b)

    def half(chip, which):
        at = pl.ds(pl.multiple_of(which * rows, rows), rows)
        return jnp.dot(held[chip, at, :], wbf[...], preferred_element_type=F32)

    def multiply(chip):
        theirs[chip] = half(chip, other).astype(BF16)
        send(theirs.at[chip], inbox.at[chip], pair_send.at[chip], pair_recv.at[chip], other, b)
        mine[chip] = half(chip, t)

    def give_sum(chip):
        done(inbox.at[chip], pair_recv.at[chip])
        summed[chip] = (mine[chip] + inbox[chip].astype(F32)).astype(BF16)
        bb = 2 * chip + t
        for stays, dst, rsem in ((True, ret_ref, ret_recv), (False, layover, lay_recv)):
            right = (home == t) if stays else (home != t)

            @pl.when(jnp.logical_and(right, bb == b))
            def _():
                pltpu.make_async_copy(summed.at[chip], features(dst, slot), rsem.at[slot]).start()

            @pl.when(jnp.logical_and(right, bb != b))
            def _():
                send(summed.at[chip], features(dst, slot), sum_send.at[chip], rsem.at[slot], t, bb)

    def pass_sum(chip):
        for core in range(2):
            bb = 2 * chip + core
            j = bb % per

            @pl.when(jnp.logical_and(c == t, bb // per != t))
            def _():
                done(layover.at[j], lay_recv.at[j])
                send(layover.at[j], features(ret_ref, j), lay_send.at[j], ret_recv.at[j], other, b)

    def add_weight(chip):
        for core in range(2):
            bb = 2 * chip + core

            @pl.when(jnp.logical_not(lands_here(bb)))
            def _():
                done(block(xall, bb), x_recv.at[bb])

        def step(i, carry):
            at = pl.ds(pl.multiple_of(i * wide, wide), wide)
            wsum_ref[at, :] += lax.dot_general(
                held[chip, :, at], xall[chip], (((0,), (0,)), ((), ())), preferred_element_type=F32
            )
            return carry

        lax.fori_loop(0, outs // wide, step, 0)

    own_copy.wait()
    done(block(held, b), own_sem.at[1])
    multiply(q)

    @pl.when(odd)
    def _():
        done(guest, swap.at[1])
        give_columns(guest)

    pass_columns(q)

    def hop(k, carry):
        for h in range(parts):
            for d in range(2):
                here = piece(origin(d, k + 1), c, h)

                @pl.when(k < count(d, c))
                def _():
                    done(here, ring_recv.at[d, k, h])

                    @pl.when(k + 1 < count(d, c))
                    def _():
                        send(here, here, ring_send.at[d, k + 1, h], ring_recv.at[d, k + 1, h], t, ahead[d])

                    send(here, here, sib_send.at[d, k, h], sib_recv.at[d, k, h], t, 2 * q + 1 - c)
        each(k, give_sum)
        each(k + 1, pass_columns)
        for d in range(2):
            @pl.when(k < count(d, 1 - c))
            def _():
                for h in range(parts):
                    done(piece(origin(d, k + 1), 1 - c, h), sib_recv.at[d, k, h])
        each(k + 1, multiply)

        @pl.when(k > 0)
        def _():
            each(k - 1, pass_sum)

        each(k, add_weight)
        return carry

    lax.fori_loop(0, hops, hop, 0)
    each(hops, give_sum)
    each(hops - 1, pass_sum)
    each(hops, add_weight)
    each(hops, pass_sum)

    smalls[b] = small_ref[...]

    def take_small(bb, carry):
        @pl.when(bb != b)
        def _():
            done(smalls.at[bb], small_recv.at[bb])
            done(small_ref, small_send.at[bb])

        return carry

    lax.fori_loop(0, nb, take_small, 0)
    total_ref[...] = jnp.sum(smalls[...], axis=0)

    @pl.when(odd)
    def _():
        done(cols_ref, swap.at[0])

    def sent_columns(j, carry):
        @pl.when(side * per + j != b)
        def _():
            done(features(cols_ref, j), x_send.at[j])

        return carry

    lax.fori_loop(0, per, sent_columns, 0)

    def sent_on(bb, carry):
        @pl.when(lands_here(bb))
        def _():
            done(block(xall, bb), x_on.at[bb])

        return carry

    lax.fori_loop(0, nb, sent_on, 0)

    def sent_sums(chip, carry):
        done(theirs.at[chip], pair_send.at[chip])

        @pl.when(2 * chip + t != b)
        def _():
            done(summed.at[chip], sum_send.at[chip])

        return carry

    lax.fori_loop(0, nc, sent_sums, 0)

    def came(j, carry):
        done(features(ret_ref, j), ret_recv.at[j])

        @pl.when(c == t)
        def _():
            done(layover.at[j], lay_send.at[j])

        return carry

    lax.fori_loop(0, per, came, 0)
    done(pre_ref, own_sem.at[0])

    def sent_pieces(k, carry):
        for h in range(parts):
            for d in range(2):
                @pl.when(k < count(d, c))
                def _():
                    done(piece(origin(d, k), c, h), ring_send.at[d, k, h])
                    done(piece(origin(d, k + 1), c, h), sib_send.at[d, k, h])

        return carry

    lax.fori_loop(0, hops, sent_pieces, 0)


def run_exchange(nb, x_first, pre_act, cotangent, gamma, columns, weight):
    rows, outs = x_first.shape
    cols = weight.shape[1]
    nc, per, hops = nb // 2, nb // 2, nb // 4
    parts = 8 if rows % 128 == 0 else 4 if rows % 64 == 0 else 1
    dma = pltpu.SemaphoreType.DMA
    vmem = pl.BlockSpec(memory_space=pltpu.VMEM)
    return pl.pallas_call(
        functools.partial(exchange, nb, parts),
        out_shape=(
            jax.ShapeDtypeStruct((rows, outs), BF16),
            jax.ShapeDtypeStruct((outs, cols), F32),
            jax.ShapeDtypeStruct(columns.shape, BF16),
            jax.ShapeDtypeStruct((2, outs), F32),
        ),
        in_specs=[vmem] * 5 + [pl.BlockSpec(memory_space=pl.ANY)],
        out_specs=(vmem,) * 4,
        scratch_shapes=[
            pltpu.VMEM((rows, outs), BF16),
            pltpu.VMEM((nc, 2 * rows, outs), BF16),
            pltpu.VMEM((nc, 2 * rows, cols), BF16),
            pltpu.VMEM((nc, rows, cols), F32),
            pltpu.VMEM((nc, rows, cols), BF16),
            pltpu.VMEM((nc, rows, cols), BF16),
            pltpu.VMEM((nc, rows, cols), BF16),
            pltpu.VMEM((per, rows, cols), BF16),
            pltpu.VMEM(columns.shape, BF16),
            pltpu.VMEM((2, outs), F32),
            pltpu.VMEM((nb, 2, outs), F32),
            pltpu.VMEM((outs, cols), F32),
            pltpu.VMEM((outs, cols), BF16),
            dma((2, hops, parts)),
            dma((2, hops, parts)),
            dma((2, hops, parts)),
            dma((2, hops, parts)),
            dma((3,)),
            dma((per,)),
            dma((nb,)),
            dma((nb,)),
            dma((2,)),
            dma((nc,)),
            dma((nc,)),
            dma((nc,)),
            dma((per,)),
            dma((per,)),
            dma((per,)),
            dma((nb,)),
            dma((nb,)),
            dma,
        ],
        compiler_params=pltpu.CompilerParams(
            collective_id=0, has_side_effects=True, vmem_limit_bytes=60 * 1024 * 1024
        ),
    )(x_first, pre_act, cotangent, gamma, columns, weight)


def shards(nb, x_first, x_layer, pre_act, gamma, weight, cotangent):
    rows = x_layer.shape[0]
    per, cols = nb // 2, weight.shape[1]
    aligned = cols % 128 == 0
    columns = x_layer if aligned else x_layer.reshape(rows, per, cols).transpose(1, 0, 2)
    grad_first, grad_weight, share, total = run_exchange(
        nb, x_first, pre_act, cotangent, gamma[None], columns, weight
    )
    if not aligned:
        share = share.transpose(1, 0, 2).reshape(rows, per * cols)
    grad_layer = (cotangent.astype(F32) + share.astype(F32)).astype(BF16)
    return (grad_first, grad_layer, grad_weight, total[0], total[1])


def solution(mesh):
    assert mesh.shape["table"] == 2 and mesh.shape["batch"] % 4 == 0
    placed = (
        P("batch", "table"),
        P("batch", "table"),
        P("batch", "table"),
        P("table"),
        P("table", "batch"),
        P("batch", "table"),
    )
    return jax.shard_map(
        functools.partial(shards, mesh.shape["batch"]),
        mesh=mesh,
        in_specs=placed,
        out_specs=(
            P("batch", "table"),
            P("batch", "table"),
            P("table", "batch"),
            P("table"),
            P("table"),
        ),
        check_vma=False,
    )
```

```python
import functools

import jax
import jax.numpy as jnp
from jax import lax
from jax.experimental import pallas as pl
from jax.experimental.pallas import tpu as pltpu
from jax.sharding import PartitionSpec as P

MESH = pl.DeviceIdType.MESH
F32 = jnp.float32
BF16 = jnp.bfloat16


def exchange(
    nb, parts,
    x_ref, act_ref, cot_ref, gamma_ref, cols_ref, weight_ref,
    first_ref, wsum_ref, ret_ref, total_ref,
    pre_ref, held, xall, mine, theirs, inbox, summed, layover, guest, small_ref, smalls, wfull, wbf,
    ring_send, ring_recv, sib_send, sib_recv, own_sem, x_send, x_on, x_recv, swap,
    pair_send, pair_recv, sum_send, lay_recv, lay_send, ret_recv, small_send, small_recv, w_sem,
):
    rows, outs = x_ref.shape
    per = nb // 2
    nc = nb // 2
    hops = nc // 2
    part = rows // parts
    t, b = lax.axis_index("table"), lax.axis_index("batch")
    q, c = b // 2, b % 2
    other = 1 - t

    def chip_at(p):
        p = (p + nc) % nc
        return jnp.where(p < hops, 2 * p, 2 * (nc - 1 - p) + 1)

    p = jnp.where(q % 2 == 0, q // 2, nc - 1 - q // 2)
    ahead = [2 * chip_at(p + 1) + c, 2 * chip_at(p - 1) + c]
    origin = lambda d, k: chip_at(p - k if d == 0 else p + k)
    count = lambda d, core: jnp.where(core == d, hops, hops - 1)
    home = b // per
    slot = b % per

    def piece(chip, core, h):
        return held.at[chip, pl.ds(pl.multiple_of(core * rows + h * part, part), part), :]

    def block(ref, bb):
        return ref.at[bb // 2, pl.ds(pl.multiple_of((bb % 2) * rows, rows), rows), :]

    def features(ref, j):
        cols = wfull.shape[1]
        return ref.at[j] if len(ref.shape) == 3 else ref.at[:, pl.ds(pl.multiple_of(j * cols, cols), cols)]

    def done(ref, sem):
        pltpu.make_async_copy(ref, ref, sem).wait()

    def send(src, dst, ssem, rsem, tt, bb):
        return pltpu.make_async_remote_copy(
            src_ref=src, dst_ref=dst, send_sem=ssem, recv_sem=rsem, device_id=(tt, bb), device_id_type=MESH
        ).start()

    def each(k, act):
        act(origin(0, k))

        @pl.when(jnp.logical_and(k > 0, k < hops))
        def _():
            act(origin(1, k))

    load_w = pltpu.make_async_copy(weight_ref, wfull, w_sem)
    load_w.start()
    barrier = pltpu.get_barrier_semaphore()

    def greet(i, carry):
        tt, bb = i // nb, i % nb

        @pl.when(jnp.logical_or(tt != t, bb != b))
        def _():
            pl.semaphore_signal(barrier, inc=1, device_id=(tt, bb), device_id_type=MESH)

        return carry

    lax.fori_loop(0, 2 * nb, greet, 0)
    small_ref[...] = jnp.zeros_like(small_ref)
    wide = 512 if outs % 512 == 0 else outs

    def gate(i, carry):
        at = pl.ds(pl.multiple_of(i * part, part), part)
        for lane in range(0, outs, wide):
            to = pl.ds(lane, wide)
            sharp = gamma_ref[:, to]
            act = act_ref[at, to].astype(F32)
            cot = cot_ref[at, to].astype(F32)
            tanh = jnp.tanh(sharp * act)
            hidden = cot * x_ref[at, to].astype(F32)
            slope = 1.0 - tanh * tanh
            first_ref[at, to] = (cot * (act * tanh)).astype(BF16)
            pre = (hidden * (tanh + sharp * act * slope)).astype(BF16)
            pre_ref[at, to] = pre
            small_ref[0:1, to] += jnp.sum(pre.astype(F32), axis=0, keepdims=True)
            small_ref[1:2, to] += jnp.sum(hidden * act * act * slope, axis=0, keepdims=True)
        return carry

    lax.fori_loop(0, parts, gate, 0)
    pl.semaphore_wait(barrier, 2 * nb - 1)

    for h in range(parts):
        start = pre_ref.at[pl.ds(h * part, part), :]
        for d in range(2):
            @pl.when(count(d, c) > 0)
            def _():
                send(start, piece(q, c, h), ring_send.at[d, 0, h], ring_recv.at[d, 0, h], t, ahead[d])
    send(pre_ref, block(held, b), own_sem.at[0], own_sem.at[1], t, 2 * q + 1 - c)
    own_copy = pltpu.make_async_copy(pre_ref, block(held, b), own_sem.at[2])
    own_copy.start()

    odd = b % 2 == 1
    side = jnp.where(odd, other, t)

    def give_columns(source):
        def give(j, carry):
            at = (j + slot) % per
            bb = side * per + at

            @pl.when(bb == b)
            def _():
                pltpu.make_async_copy(features(source, at), block(xall, b), x_recv.at[b]).start()

            @pl.when(bb != b)
            def _():
                send(features(source, at), block(xall, b), x_send.at[at], x_recv.at[b], t, bb)

            return carry

        lax.fori_loop(0, per, give, 0)

    @pl.when(odd)
    def _():
        send(cols_ref, guest, swap.at[0], swap.at[1], other, b)

    @pl.when(jnp.logical_not(odd))
    def _():
        give_columns(cols_ref)

    def give_small(bb, carry):
        @pl.when(bb != b)
        def _():
            send(small_ref, smalls.at[b], small_send.at[bb], small_recv.at[b], t, bb)

        return carry

    lax.fori_loop(0, nb, give_small, 0)
    load_w.wait()
    wbf[...] = wfull[...].astype(BF16)
    wsum_ref[...] = jnp.zeros_like(wsum_ref)

    def lands_here(bb):
        return (home + bb) % 2 == t

    def pass_columns(chip):
        for core in range(2):
            bb = 2 * chip + core

            @pl.when(lands_here(bb))
            def _():
                done(block(xall, bb), x_recv.at[bb])
                send(block(xall, bb), block(xall, bb), x_on.at[bb], x_recv.at[bb], other, b)

    def half(chip, which):
        at = pl.ds(pl.multiple_of(which * rows, rows), rows)
        return jnp.dot(held[chip, at, :], wbf[...], preferred_element_type=F32)

    def multiply(chip):
        theirs[chip] = half(chip, other).astype(BF16)
        send(theirs.at[chip], inbox.at[chip], pair_send.at[chip], pair_recv.at[chip], other, b)
        mine[chip] = half(chip, t)

    def give_sum(chip):
        done(inbox.at[chip], pair_recv.at[chip])
        summed[chip] = (mine[chip] + inbox[chip].astype(F32)).astype(BF16)
        bb = 2 * chip + t
        for stays, dst, rsem in ((True, ret_ref, ret_recv), (False, layover, lay_recv)):
            right = (home == t) if stays else (home != t)

            @pl.when(jnp.logical_and(right, bb == b))
            def _():
                pltpu.make_async_copy(summed.at[chip], features(dst, slot), rsem.at[slot]).start()

            @pl.when(jnp.logical_and(right, bb != b))
            def _():
                send(summed.at[chip], features(dst, slot), sum_send.at[chip], rsem.at[slot], t, bb)

    def pass_sum(chip):
        for core in range(2):
            bb = 2 * chip + core
            j = bb % per

            @pl.when(jnp.logical_and(c == t, bb // per != t))
            def _():
                done(layover.at[j], lay_recv.at[j])
                send(layover.at[j], features(ret_ref, j), lay_send.at[j], ret_recv.at[j], other, b)

    def add_weight(chip):
        for core in range(2):
            bb = 2 * chip + core

            @pl.when(jnp.logical_not(lands_here(bb)))
            def _():
                done(block(xall, bb), x_recv.at[bb])

        def step(i, carry):
            at = pl.ds(pl.multiple_of(i * wide, wide), wide)
            wsum_ref[at, :] += lax.dot_general(
                held[chip, :, at], xall[chip], (((0,), (0,)), ((), ())), preferred_element_type=F32
            )
            return carry

        lax.fori_loop(0, outs // wide, step, 0)

    own_copy.wait()
    done(block(held, b), own_sem.at[1])
    multiply(q)

    @pl.when(odd)
    def _():
        done(guest, swap.at[1])
        give_columns(guest)

    pass_columns(q)

    def hop(k, carry):
        for h in range(parts):
            for d in range(2):
                here = piece(origin(d, k + 1), c, h)

                @pl.when(k < count(d, c))
                def _():
                    done(here, ring_recv.at[d, k, h])

                    @pl.when(k + 1 < count(d, c))
                    def _():
                        send(here, here, ring_send.at[d, k + 1, h], ring_recv.at[d, k + 1, h], t, ahead[d])

                    send(here, here, sib_send.at[d, k, h], sib_recv.at[d, k, h], t, 2 * q + 1 - c)
        each(k, give_sum)
        each(k + 1, pass_columns)
        for d in range(2):
            @pl.when(k < count(d, 1 - c))
            def _():
                for h in range(parts):
                    done(piece(origin(d, k + 1), 1 - c, h), sib_recv.at[d, k, h])
        each(k + 1, multiply)

        @pl.when(k > 0)
        def _():
            each(k - 1, pass_sum)

        @pl.when(k < hops - 1)
        def _():
            each(k, add_weight)

        return carry

    lax.fori_loop(0, hops, hop, 0)
    each(hops, give_sum)
    each(hops - 1, pass_sum)
    each(hops - 1, add_weight)
    each(hops, add_weight)
    each(hops, pass_sum)

    smalls[b] = small_ref[...]

    def take_small(bb, carry):
        @pl.when(bb != b)
        def _():
            done(smalls.at[bb], small_recv.at[bb])
            done(small_ref, small_send.at[bb])

        return carry

    lax.fori_loop(0, nb, take_small, 0)
    total_ref[...] = jnp.sum(smalls[...], axis=0)

    @pl.when(odd)
    def _():
        done(cols_ref, swap.at[0])

    def sent_columns(j, carry):
        @pl.when(side * per + j != b)
        def _():
            done(features(cols_ref, j), x_send.at[j])

        return carry

    lax.fori_loop(0, per, sent_columns, 0)

    def sent_on(bb, carry):
        @pl.when(lands_here(bb))
        def _():
            done(block(xall, bb), x_on.at[bb])

        return carry

    lax.fori_loop(0, nb, sent_on, 0)

    def sent_sums(chip, carry):
        done(theirs.at[chip], pair_send.at[chip])

        @pl.when(2 * chip + t != b)
        def _():
            done(summed.at[chip], sum_send.at[chip])

        return carry

    lax.fori_loop(0, nc, sent_sums, 0)

    def came(j, carry):
        done(features(ret_ref, j), ret_recv.at[j])

        @pl.when(c == t)
        def _():
            done(layover.at[j], lay_send.at[j])

        return carry

    lax.fori_loop(0, per, came, 0)
    done(pre_ref, own_sem.at[0])

    def sent_pieces(k, carry):
        for h in range(parts):
            for d in range(2):
                @pl.when(k < count(d, c))
                def _():
                    done(piece(origin(d, k), c, h), ring_send.at[d, k, h])
                    done(piece(origin(d, k + 1), c, h), sib_send.at[d, k, h])

        return carry

    lax.fori_loop(0, hops, sent_pieces, 0)


def run_exchange(nb, x_first, pre_act, cotangent, gamma, columns, weight):
    rows, outs = x_first.shape
    cols = weight.shape[1]
    nc, per, hops = nb // 2, nb // 2, nb // 4
    parts = 8 if rows % 128 == 0 else 4 if rows % 64 == 0 else 1
    dma = pltpu.SemaphoreType.DMA
    vmem = pl.BlockSpec(memory_space=pltpu.VMEM)
    return pl.pallas_call(
        functools.partial(exchange, nb, parts),
        out_shape=(
            jax.ShapeDtypeStruct((rows, outs), BF16),
            jax.ShapeDtypeStruct((outs, cols), F32),
            jax.ShapeDtypeStruct(columns.shape, BF16),
            jax.ShapeDtypeStruct((2, outs), F32),
        ),
        in_specs=[vmem] * 5 + [pl.BlockSpec(memory_space=pl.ANY)],
        out_specs=(vmem,) * 4,
        scratch_shapes=[
            pltpu.VMEM((rows, outs), BF16),
            pltpu.VMEM((nc, 2 * rows, outs), BF16),
            pltpu.VMEM((nc, 2 * rows, cols), BF16),
            pltpu.VMEM((nc, rows, cols), F32),
            pltpu.VMEM((nc, rows, cols), BF16),
            pltpu.VMEM((nc, rows, cols), BF16),
            pltpu.VMEM((nc, rows, cols), BF16),
            pltpu.VMEM((per, rows, cols), BF16),
            pltpu.VMEM(columns.shape, BF16),
            pltpu.VMEM((2, outs), F32),
            pltpu.VMEM((nb, 2, outs), F32),
            pltpu.VMEM((outs, cols), F32),
            pltpu.VMEM((outs, cols), BF16),
            dma((2, hops, parts)),
            dma((2, hops, parts)),
            dma((2, hops, parts)),
            dma((2, hops, parts)),
            dma((3,)),
            dma((per,)),
            dma((nb,)),
            dma((nb,)),
            dma((2,)),
            dma((nc,)),
            dma((nc,)),
            dma((nc,)),
            dma((per,)),
            dma((per,)),
            dma((per,)),
            dma((nb,)),
            dma((nb,)),
            dma,
        ],
        compiler_params=pltpu.CompilerParams(
            collective_id=0, has_side_effects=True, vmem_limit_bytes=60 * 1024 * 1024
        ),
    )(x_first, pre_act, cotangent, gamma, columns, weight)


def shards(nb, x_first, x_layer, pre_act, gamma, weight, cotangent):
    rows = x_layer.shape[0]
    per, cols = nb // 2, weight.shape[1]
    aligned = cols % 128 == 0
    columns = x_layer if aligned else x_layer.reshape(rows, per, cols).transpose(1, 0, 2)
    grad_first, grad_weight, share, total = run_exchange(
        nb, x_first, pre_act, cotangent, gamma[None], columns, weight
    )
    if not aligned:
        share = share.transpose(1, 0, 2).reshape(rows, per * cols)
    grad_layer = (cotangent.astype(F32) + share.astype(F32)).astype(BF16)
    return (grad_first, grad_layer, grad_weight, total[0], total[1])


def solution(mesh):
    assert mesh.shape["table"] == 2 and mesh.shape["batch"] % 4 == 0
    placed = (
        P("batch", "table"),
        P("batch", "table"),
        P("batch", "table"),
        P("table"),
        P("table", "batch"),
        P("batch", "table"),
    )
    return jax.shard_map(
        functools.partial(shards, mesh.shape["batch"]),
        mesh=mesh,
        in_specs=placed,
        out_specs=(
            P("batch", "table"),
            P("batch", "table"),
            P("table", "batch"),
            P("table"),
            P("table"),
        ),
        check_vma=False,
    )
```
